32 devices in a mesh: leaf: 16 (over z, y, x), sub: 2 (over core).
Axes of the slice: x: 2, y: 2, z: 4, core: 2. Of those that a mesh axis runs over, the one named last changes fastest.
Arguments:
- points: float32 [2, 262144], P(None, ('leaf', 'sub')), may hold values from 0 to 1
- right_sides: float32 [32, 262144], P(None, ('leaf', 'sub')), may hold values from -0.6 to 0.6
- leaf_order: int32 [2048], P(('leaf', 'sub')), may hold values from 0 to 63, as said below
- leaf_basis: float32 [2048, 32, 128], P(('leaf', 'sub')), may hold values from -0.5 to 0.5
- transfer_low: float32 [512, 32, 128], P(('leaf', 'sub')), may hold values from -0.5 to 0.5
- transfer_top: float32 [512, 32, 32], P(('leaf', 'sub')), may hold values from -0.1875 to 0.1875
- proxy_low: float32 [512, 2, 32], P(('leaf', 'sub')), may hold values from 0 to 1
- proxy_top: float32 [16, 2, 32], replicated, may hold values from 0 to 1
- near_lists: int32 [2048, 9], P(('leaf', 'sub')), may hold values from 0 to 2047, as said below
- far_lists: int32 [512, 27], P(('leaf', 'sub')), may hold values from 0 to 511, as said below
- top_lists: int32 [16, 27], P('leaf'), may hold values from 0 to 15
- subtree_map: int32 [16], replicated, may hold values from 0 to 15, each once
Outputs:
- product: float32 [32, 262144], P(None, ('leaf', 'sub'))
The draws below stay inside these ranges and needn't reach their ends.
Inputs may be any that keep to these rules, and one draw needn't show every extreme that they name: `leaf_order`: each device's block of 64 entries is a permutation of 0 to 63. `near_lists`: entries are global leaf numbers; leaf s lies on device s // 64, devices numbered leaf index times the size of sub plus sub index and laid out in rows of 16. Of the entries of one device's leaves exactly 256 lie on other devices, all on the devices beside it in its row or in its column (number one less or one more in the same row of 16, or 16 less or 16 more), at most 128 on any one of them, and for every device some such neighbour holds exactly 128. `far_lists`: entries are global cluster numbers; cluster s lies on device s // 16, and the sources of a device's clusters lie on that device or on the devices numbered one less or one more.
All inputs are finite; a program needn't handle non-finite values.
Results may differ from the reference program's by a relative error of at most 0.00017.
Values sent between devices are 32-bit elements; how exact they have to be, the bound alone decides.
A program may use at most 128 MiB of HBM per device.

```python
import jax
import jax.numpy as jnp
from jax import lax

LEAF = 128
RANK = 32
RHS = 32
LPD = 64
NEAR = 9
FAR1 = 27
FAR2 = 27
CAP = 128
NPTS = 262144
NLEAVES = 2048
NC_DEV = 16
NC1 = 512
SUBTREES = 16
REMOTE = 256


def draw_leaf_order(key, part):
    device_count = NLEAVES // LPD
    device_keys = jax.random.split(jax.random.fold_in(key, 3), device_count)
    blocks = jax.vmap(lambda single: jax.random.permutation(single, LPD))(device_keys)
    return blocks.reshape(-1).astype(jnp.int32)


def near_block(single, device):
    device_count = NLEAVES // LPD
    row_count = device_count // 16
    task_count = LPD * NEAR
    first_key, second, third, fourth = jax.random.split(single, 4)
    column = device % 16
    row_number = device // 16
    offsets = jnp.array([-16, -1, 1, 16], dtype=jnp.int32)
    valid = jnp.stack([row_number > 0, column > 0, column < 15, row_number < row_count - 1]).astype(jnp.int32)
    forced = jnp.argmax(valid).astype(jnp.int32)
    slot_ids = jnp.arange(4 * CAP, dtype=jnp.int32)
    neighbour = slot_ids // CAP
    scores = jax.random.permutation(first_key, 4 * CAP).astype(jnp.int32)
    scores = jnp.where(neighbour == forced, -1, scores)
    scores = jnp.where(valid[neighbour] == 0, 8 * CAP, scores)
    chosen = jnp.argsort(scores, stable=True)[:REMOTE].astype(jnp.int32)
    owners = device + offsets[chosen // CAP]
    remote = owners * LPD + jax.random.randint(second, (REMOTE,), 0, LPD)
    local_ids = device * LPD + jax.random.randint(third, (task_count - REMOTE,), 0, LPD)
    joined = jnp.concatenate([remote, local_ids]).astype(jnp.int32)
    return joined[jax.random.permutation(fourth, task_count)].reshape(LPD, NEAR)


def draw_near_lists(key, part):
    device_count = NLEAVES // LPD
    device_keys = jax.random.split(jax.random.fold_in(key, 7), device_count)
    blocks = jax.vmap(near_block)(device_keys, jnp.arange(device_count, dtype=jnp.int32))
    return blocks.reshape(NLEAVES, NEAR).astype(jnp.int32)


def draw_far_lists(key, part):
    first_key, second = jax.random.split(jax.random.fold_in(key, 11))
    device = jnp.arange(NC1, dtype=jnp.int32)[:, None] // NC_DEV
    offset = jax.random.randint(first_key, (NC1, FAR1), -1, 2)
    chosen = jnp.clip(device + offset, 0, NC1 // NC_DEV - 1)
    return (chosen * NC_DEV + jax.random.randint(second, (NC1, FAR1), 0, NC_DEV)).astype(jnp.int32)


def plant(values, stream_key, smallest, largest):
    extent = values.shape
    place = [jax.random.randint(jax.random.fold_in(stream_key, axis), (), 0, extent[axis]) for axis in range(len(extent))]
    values = values.at[tuple(place)].set(smallest)
    longest = extent.index(max(extent))
    place[longest] = (place[longest] + 1) % extent[longest]
    return values.at[tuple(place)].set(largest)


def shard_levels(own_key, shape, cuts, least, top_value):
    gain = 1.0
    for position, parts in cuts:
        draws = jax.random.uniform(jax.random.fold_in(jax.random.fold_in(own_key, 6), position), (parts,), jnp.float32, least / len(cuts), top_value / len(cuts))
        gain = gain * jnp.repeat(jnp.exp(draws), shape[position] // parts).reshape((-1,) + (1,) * (len(shape) - 1 - position))
    return gain


def noise(rng, shape, deviation, limit, cuts=(), held_as=jnp.bfloat16):
    values = jax.random.normal(rng, shape, jnp.float32) * deviation
    if len(cuts) > 0:
        values = shard_levels(rng, shape, cuts, -0.22, 0.18) * values
    return jnp.clip(values, min=-limit, max=limit).astype(held_as)


def setup_inputs(seed: int = 0) -> dict:
    splits = jax.random.split(jax.random.key(seed), 13)
    return {
        "points": jnp.clip(1.0 * jax.random.uniform(splits[0], (2, NPTS), jnp.float32) ** shard_levels(splits[0], (2, NPTS), ((1, 32),), -0.2, 0.2), 0.0, 1.0),
        "right_sides": noise(splits[1], (RHS, NPTS), 0.1, 0.6, ((1, 32),), jnp.float32),
        "leaf_order": draw_leaf_order(jax.random.fold_in(splits[12], 71), 0),
        "leaf_basis": noise(splits[3], (NLEAVES, RANK, LEAF), LEAF ** -0.5, 0.5, ((0, 32),), jnp.float32),
        "transfer_low": noise(splits[4], (NC1, RANK, 4 * RANK), (4 * RANK) ** -0.5, 0.5, ((0, 32),), jnp.float32),
        "transfer_top": noise(splits[5], (NC1, RANK, RANK), (2 * RANK * NC_DEV) ** -0.5, 0.1875, ((0, 32),), jnp.float32),
        "proxy_low": jnp.clip(1.0 * jax.random.uniform(splits[6], (NC1, 2, RANK), jnp.float32) ** shard_levels(splits[6], (NC1, 2, RANK), ((0, 32),), -0.2, 0.2), 0.0, 1.0),
        "proxy_top": jnp.clip(jax.random.uniform(splits[7], (SUBTREES, 2, RANK), jnp.float32, 0.0, 1.0), 0.0, 1.0),
        "near_lists": draw_near_lists(jax.random.fold_in(splits[12], 71), 0),
        "far_lists": draw_far_lists(jax.random.fold_in(splits[12], 71), 0),
        "top_lists": plant(jax.random.randint(splits[10], (SUBTREES, FAR2), 0, SUBTREES), jax.random.fold_in(splits[10], 1), 0, SUBTREES - 1).astype(jnp.int32),
        "subtree_map": jax.random.permutation(splits[11], SUBTREES).astype(jnp.int32),
    }


length_scale = 0.25
highest = lax.Precision.HIGHEST

def kernel_block(first_points, second):
    delta_x = first_points[..., 0, :, None] - second[..., 0, None, :]
    delta_y = first_points[..., 1, :, None] - second[..., 1, None, :]
    return jnp.exp(-jnp.sqrt(delta_x * delta_x + delta_y * delta_y) / length_scale)

def reference(points, right_sides, leaf_order, leaf_basis, transfer_low, transfer_top, proxy_low, proxy_top, near_lists, far_lists, top_lists, subtree_map):
    leaf_ids = jnp.arange(NLEAVES, dtype=jnp.int32)
    source_block = (leaf_order + leaf_ids // LPD * LPD).astype(jnp.int32)
    leaf_xy = points.reshape(2, NLEAVES, LEAF).transpose(1, 0, 2)[source_block]
    leaf_values = right_sides.reshape(RHS, NLEAVES, LEAF).transpose(1, 0, 2)[source_block]
    coef_leaf = jnp.einsum('bql,brl->bqr', leaf_values, leaf_basis, precision=highest)
    stacked = coef_leaf.reshape(NC1, 4, RHS, RANK).transpose(0, 2, 1, 3).reshape(NC1, RHS, 4 * RANK)
    coef_low = jnp.einsum('cqk,crk->cqr', stacked, transfer_low, precision=highest)
    coef_top = jnp.einsum('cqr,crs->cqs', coef_low, transfer_top, precision=highest)
    coef_top = coef_top.reshape(SUBTREES, NC1 // SUBTREES, RHS, RANK).sum(axis=1)
    source_chips = subtree_map[top_lists]
    coupling_top = kernel_block(proxy_top[:, None], proxy_top[source_chips])
    down_top = jnp.einsum('akqs,akts->aqt', coef_top[source_chips], coupling_top, precision=highest)

    def cluster_down(cluster_id):
        source_ids = far_lists[cluster_id]
        coupling = kernel_block(proxy_low[cluster_id], proxy_low[source_ids])
        return jnp.einsum('kqs,kts->qt', coef_low[source_ids], coupling, precision=highest)
    down_low = lax.map(cluster_down, jnp.arange(NC1, dtype=jnp.int32), batch_size=256)
    chip_of = jnp.arange(NC1, dtype=jnp.int32) // (NC1 // SUBTREES)
    down_low = down_low + jnp.einsum('cqs,crs->cqr', down_top[chip_of], transfer_top, precision=highest)
    down_stack = jnp.einsum('cqr,crk->cqk', down_low, transfer_low, precision=highest)
    down_leaf = down_stack.reshape(NC1, RHS, 4, RANK).transpose(0, 2, 1, 3).reshape(NLEAVES, RHS, RANK)
    far_part = jnp.einsum('bqr,brl->bql', down_leaf, leaf_basis, precision=highest)

    def leaf_near(leaf_id):
        source_ids = near_lists[leaf_id]
        kernel = kernel_block(leaf_xy[leaf_id], leaf_xy[source_ids])
        return jnp.einsum('kqj,kij->qi', leaf_values[source_ids], kernel, precision=highest)
    near_part = lax.map(leaf_near, leaf_ids, batch_size=16)
    leaf_result = far_part + near_part
    placed = jnp.zeros_like(leaf_result).at[source_block].set(leaf_result)
    return placed.transpose(1, 0, 2).reshape(RHS, NPTS)
```

```python
import functools

import jax
import jax.numpy as jnp
from jax import lax
from jax.experimental import pallas as pl
from jax.experimental.pallas import tpu as pltpu
from jax.sharding import PartitionSpec as P

LEAF = 128
RANK = 32
RHS = 32
NEAR = 9
CAP = 128
ROW = 16
GROUP = 8
length_scale = 0.25
log2e = 1.4426950408889634
scale = log2e / length_scale
highest = lax.Precision.HIGHEST
NT = (((1,), (1,)), ((), ()))
NN = (((1,), (0,)), ((), ()))
MESH = pl.DeviceIdType.MESH
f32 = jnp.float32
bf16 = jnp.bfloat16
smem = pl.BlockSpec(memory_space=pltpu.SMEM)
vmem = pl.BlockSpec(memory_space=pltpu.VMEM)


def dot_full(a, b, dims):
    return lax.dot_general(a, b, dims, precision=highest, preferred_element_type=f32)


def split(x):
    high = x.astype(bf16)
    return high, (x - high.astype(f32)).astype(bf16)


def dot_split(stacked, count, kernel):
    high, low = split(kernel)
    first = lax.dot_general(stacked, high, NT, preferred_element_type=f32)
    second = lax.dot_general(stacked[:count], low, NT, preferred_element_type=f32)
    return first[:count] + first[count:] + second


def kern(px, py, qx, qy):
    dx = px - qx
    dy = py - qy
    square = jnp.maximum(dx * dx + dy * dy, 1e-30)
    return jnp.exp2(-(square * lax.rsqrt(square)))


def up_kernel(order, rhs, basis, low, top, proxy, packed, partial):
    clusters = low.shape[0]
    partial[...] = jnp.zeros_like(partial)
    packed[:, RHS:, :] = jnp.zeros((clusters, 8, RANK), f32)
    packed[:, RHS : RHS + 2, :] = proxy[...] * scale

    def step(i, total):
        for j in range(2):
            c = i * 2 + j
            parts = []
            for m in range(4):
                leaf = c * 4 + m
                block = rhs[:, pl.ds(pl.multiple_of(order[leaf] * LEAF, LEAF), LEAF)]
                parts.append(dot_full(block, basis[leaf], NT))
            value = dot_full(jnp.concatenate(parts, axis=1), low[c], NT)
            packed[c, 0:RHS, :] = value
            total = total + dot_full(value, top[c], NN)
        return total

    total = lax.fori_loop(0, clusters // 2, step, jnp.zeros((RHS, RANK), f32))
    partial[...] = jnp.concatenate([total[8 * g : 8 * g + 8] for g in range(4)], axis=1)


def exchange_kernel(count, sub, packed, partial, sides, tops, side_in, slots, send, recv, side_send, side_recv):
    me = lax.axis_index("leaf") * sub + lax.axis_index("sub")

    def place(device):
        return (device // sub, device % sub)

    barrier = pltpu.get_barrier_semaphore()

    def greet(step, carry):
        pl.semaphore_signal(barrier, inc=1, device_id=place((me + step) % count), device_id_type=MESH)
        return carry

    lax.fori_loop(1, count, greet, 0)
    pl.semaphore_wait(barrier, count - 1)

    def side(number, step):
        return pltpu.make_async_remote_copy(
            src_ref=packed,
            dst_ref=side_in.at[number],
            send_sem=side_send.at[number],
            recv_sem=side_recv.at[number],
            device_id=place((me + step) % count),
            device_id_type=MESH,
        )

    def far(step):
        return pltpu.make_async_remote_copy(
            src_ref=partial,
            dst_ref=slots.at[step],
            send_sem=send.at[step],
            recv_sem=recv.at[step],
            device_id=place((me + step) % count),
            device_id_type=MESH,
        )

    def start(step, carry):
        far(step).start()
        return carry

    def finish(step, carry):
        far(step).wait()
        tops[step] = slots[step]
        return carry

    lax.fori_loop(1, count, start, 0)
    side(0, 1).start()
    side(1, count - 1).start()
    tops[0] = partial[...]
    lax.fori_loop(1, count, finish, 0)
    side(0, 1).wait()
    side(1, count - 1).wait()
    sides[...] = side_in[...]


def columns(points, order, px, py):
    def step(b, carry):
        start = pl.multiple_of(order[b] * LEAF, LEAF)
        pair = points[:, pl.ds(start, LEAF)]
        px[b] = jnp.broadcast_to(pair[0:1], (LEAF, LEAF)).T
        py[b] = jnp.broadcast_to(pair[1:2], (LEAF, LEAF)).T
        return carry

    lax.fori_loop(0, px.shape[0], step, 0, unroll=2)


def near_sum(first, last, leaves, tasks, orders, load, px, py, out):
    def step(i, carry):
        results = []
        for j in range(GROUP):
            word = tasks[first + i * GROUP + j]
            target = word % leaves
            source = word // leaves
            x, qx, qy = load(source // leaves, orders[source])
            stacked = jnp.concatenate(split(x), axis=0)
            kernel = kern(px[target], py[target], qx, qy)
            results.append((target, dot_split(stacked, RHS, kernel)))
        for target, value in results:
            place = pl.ds(pl.multiple_of(orders[target] * LEAF, LEAF), LEAF)
            out[:, place] += value
        return carry

    lax.fori_loop(0, (last - first) // GROUP, step, 0)


def home_kernel(
    local, leaves, tasks, orders, far_lists, sources, where, points, rhs, basis, low, top,
    proxy_t, proxy_top, proxy_top_t, widened_low, widened_own, tops, out, px, py, coefs, table,
):
    device, chip, count, sub = (where[i] for i in range(4))
    clusters = low.shape[0]
    far_count = far_lists.shape[0] // clusters
    columns(points, orders, px, py)
    out[...] = jnp.zeros_like(out)

    def load(number, block):
        start = pl.multiple_of(block * LEAF, LEAF)
        pair = points[:, pl.ds(start, LEAF)]
        return rhs[:, pl.ds(start, LEAF)], pair[0:1], pair[1:2]

    near_sum(0, local, leaves, tasks, orders, load, px, py, out)

    table[0:clusters] = widened_low[0]
    table[clusters : 2 * clusters] = widened_own[...]
    table[2 * clusters :] = widened_low[1]

    def join(u, carry):
        total = tops[(device - u * sub + count) % count]
        for core in range(1, tops.shape[0] // coefs.shape[0]):
            total = total + tops[(device - u * sub - core + count) % count]
        coefs[u] = jnp.concatenate([total[:, RANK * g : RANK * g + RANK] for g in range(4)], axis=0)
        return carry

    lax.fori_loop(0, coefs.shape[0], join, 0)

    own = proxy_top_t[chip]
    own_x = jnp.broadcast_to(own[:, 0:1], (RANK, RANK))
    own_y = jnp.broadcast_to(own[:, 1:2], (RANK, RANK))
    down_top = jnp.zeros((RHS, RANK), f32)
    for k in range(sources.shape[0]):
        u = sources[k]
        pair = proxy_top[u]
        stacked = jnp.concatenate(split(coefs[u]), axis=0)
        down_top += dot_split(stacked, RHS, kern(own_x, own_y, pair[0:1], pair[1:2]))

    def cluster(c, carry):
        own = proxy_t[c]
        tx = jnp.broadcast_to(own[:, 0:1], (RANK, RANK))
        ty = jnp.broadcast_to(own[:, 1:2], (RANK, RANK))
        total = dot_full(down_top, top[c], NT)
        for k in range(far_count):
            s = far_lists[c * far_count + k] - (device - 1) * clusters
            pair = table[s, RHS : RHS + 2, :]
            stacked = jnp.concatenate(split(table[s, 0:RHS, :]), axis=0)
            total += dot_split(stacked, RHS, kern(tx, ty, pair[0:1], pair[1:2]))
        down = dot_full(total, low[c], NN)
        for m in range(4):
            leaf = c * 4 + m
            place = pl.ds(pl.multiple_of(orders[leaf] * LEAF, LEAF), LEAF)
            out[:, place] += dot_full(down[:, m * RANK : (m + 1) * RANK], basis[leaf], NN)
        return carry

    lax.fori_loop(0, clusters, cluster, 0)


def away_kernel(first, last, leaves, tasks, orders, points, pieces, before, out, px, py):
    columns(points, orders, px, py)
    out[...] = before[...]
    value_rows = RHS * leaves

    def load(number, block):
        tiles = [
            pieces[number - 1, pl.ds(pl.multiple_of(tile * leaves * 8 + block * 8, 8), 8), :]
            for tile in range(RHS // 8)
        ]
        qx = pieces[number - 1, pl.ds(value_rows + block * 2, 1), :]
        qy = pieces[number - 1, pl.ds(value_rows + block * 2 + 1, 1), :]
        return jnp.concatenate(tiles, axis=0), qx, qy

    near_sum(first, last, leaves, tasks, orders, load, px, py, out)


def per_device(
    points, right_sides, leaf_order, leaf_basis, transfer_low, transfer_top, proxy_low, proxy_top,
    near_lists, far_lists, top_lists, subtree_map,
):
    chips = lax.axis_size("leaf")
    sub = lax.axis_size("sub")
    count = chips * sub
    chip = lax.axis_index("leaf").astype(jnp.int32)
    device = chip * sub + lax.axis_index("sub").astype(jnp.int32)
    leaves = leaf_order.shape[0]
    clusters = transfer_low.shape[0]
    width = leaves * LEAF
    params = functools.partial(pltpu.CompilerParams, vmem_limit_bytes=60 << 20)

    packed, partial = pl.pallas_call(
        up_kernel,
        out_shape=(
            jax.ShapeDtypeStruct((clusters, RHS + 8, RANK), f32),
            jax.ShapeDtypeStruct((8, 4 * RANK), f32),
        ),
        in_specs=[smem] + [vmem] * 5,
        out_specs=(vmem, vmem),
        compiler_params=params(),
        name="up",
    )(leaf_order, right_sides, leaf_basis, transfer_low, transfer_top, proxy_low)

    sides, tops = pl.pallas_call(
        functools.partial(exchange_kernel, count, sub),
        out_shape=(
            jax.ShapeDtypeStruct((2,) + packed.shape, f32),
            jax.ShapeDtypeStruct((count,) + partial.shape, f32),
        ),
        in_specs=[vmem, vmem],
        out_specs=(vmem, vmem),
        scratch_shapes=[
            pltpu.VMEM((2,) + packed.shape, f32),
            pltpu.VMEM((count,) + partial.shape, f32),
            pltpu.SemaphoreType.DMA((count,)),
            pltpu.SemaphoreType.DMA((count,)),
            pltpu.SemaphoreType.DMA((2,)),
            pltpu.SemaphoreType.DMA((2,)),
        ],
        compiler_params=params(collective_id=0, has_side_effects=True),
        name="exchange",
    )(packed, partial)

    scaled = points * scale
    value_rows = right_sides.reshape(RHS // 8, 8, leaves, LEAF).transpose(0, 2, 1, 3).reshape(-1, LEAF)
    point_rows = scaled.reshape(2, leaves, LEAF).transpose(1, 0, 2).reshape(-1, LEAF)
    order_rows = jnp.pad(leaf_order.astype(f32).reshape(1, leaves), ((0, 7), (0, LEAF - leaves)))
    payload = jnp.concatenate([value_rows, point_rows, order_rows], axis=0)
    payload, tops, sides = lax.optimization_barrier((payload, tops, sides))

    rows = count // ROW
    below = [(i + 1, i) for i in range(count - 1)]
    above = [(i, i + 1) for i in range(count - 1)]
    axes = ("leaf", "sub")
    moves = []
    if rows == 2:
        moves.append((lax.ppermute(payload, axes, [(i, (i + ROW) % count) for i in range(count)]), (-ROW, ROW)))
    elif rows > 2:
        moves.append((lax.ppermute(payload, axes, [(i, i + ROW) for i in range(count - ROW)]), (-ROW,)))
        moves.append((lax.ppermute(payload, axes, [(i + ROW, i) for i in range(count - ROW)]), (ROW,)))
    moves.append((lax.ppermute(payload, axes, above), (-1,)))
    moves.append((lax.ppermute(payload, axes, below), (1,)))
    moves = moves[::-1]

    flat = near_lists.reshape(-1)
    step = flat // leaves - device
    number = jnp.zeros_like(flat)
    for index, (_, steps) in enumerate(moves):
        for by in steps:
            number = jnp.where(step == by, index + 1, number)
    target = jnp.arange(flat.shape[0], dtype=jnp.int32) // NEAR
    tasks = jnp.sort((number * leaves + flat % leaves) * leaves + target)
    local = flat.shape[0] - 2 * CAP

    source_chips = subtree_map[top_lists[0]]
    where = jnp.stack([device, chip, jnp.int32(count), jnp.int32(sub)])
    home = pl.pallas_call(
        functools.partial(home_kernel, local, leaves),
        out_shape=jax.ShapeDtypeStruct((RHS, width), f32),
        in_specs=[smem] * 5 + [vmem] * 11,
        out_specs=vmem,
        scratch_shapes=[
            pltpu.VMEM((leaves, LEAF, LEAF), f32),
            pltpu.VMEM((leaves, LEAF, LEAF), f32),
            pltpu.VMEM((chips, RHS, RANK), f32),
            pltpu.VMEM((3 * clusters, RHS + 8, RANK), f32),
        ],
        compiler_params=params(),
        cost_estimate=pl.CostEstimate(flops=20_000_000_000, bytes_accessed=6_000_000, transcendentals=10_000_000),
        name="home",
    )(
        tasks, leaf_order, far_lists.reshape(-1), source_chips, where, scaled, right_sides, leaf_basis,
        transfer_low, transfer_top, proxy_low.transpose(0, 2, 1) * scale, proxy_top * scale,
        proxy_top.transpose(0, 2, 1) * scale, sides, packed, tops,
    )

    pieces = jnp.stack([piece for piece, _ in moves])
    got_orders = pieces[:, -8, :leaves].astype(jnp.int32)
    orders = jnp.concatenate([leaf_order[None], got_orders]).reshape(-1)
    return pl.pallas_call(
        functools.partial(away_kernel, local, flat.shape[0], leaves),
        out_shape=jax.ShapeDtypeStruct((RHS, width), f32),
        in_specs=[smem] * 2 + [vmem] * 3,
        out_specs=vmem,
        scratch_shapes=[pltpu.VMEM((leaves, LEAF, LEAF), f32), pltpu.VMEM((leaves, LEAF, LEAF), f32)],
        compiler_params=params(),
        cost_estimate=pl.CostEstimate(flops=10_000_000_000, bytes_accessed=6_000_000, transcendentals=8_000_000),
        name="away",
    )(tasks, orders, scaled, pieces, home)


def solution(mesh):
    both = ("leaf", "sub")
    return jax.shard_map(
        per_device,
        mesh=mesh,
        in_specs=(
            P(None, both), P(None, both), P(both), P(both, None, None), P(both, None, None),
            P(both, None, None), P(both, None, None), P(), P(both, None), P(both, None),
            P("leaf", None), P(),
        ),
        out_specs=P(None, both),
        check_vma=False,
    )
```
